32 devices in a mesh: rep: 4 (over x, core), grp: 8 (over z, y).
Axes of the slice: x: 2, y: 2, z: 4, core: 2. Of those that a mesh axis runs over, the one named last changes fastest.
Arguments:
- tokens: bfloat16 [4096, 768], P(('rep', 'grp')), may hold values from -6 to 6
- segment_ids: int32 [32, 128], P(('rep', 'grp')), may hold values from 0 to 3, never falling along the last dimension, each value on 1 to 64 neighbouring positions
- position_buckets: int32 [64], replicated, may hold values from 0 to 31
- routes: int32 [4096, 2], P(('rep', 'grp')), may hold values from 0 to 7, all different within a row; in each aligned block of 128 rows (0 to 127, 128 to 255, ...) at most 48 rows name the same one
- gates: float32 [4096, 2], P(('rep', 'grp')), may hold values from 0.1 to 0.9
- attn_gain: bfloat16 [768], P('grp'), may hold values from 0.5 to 1.5
- w_query: bfloat16 [768, 768], P('grp'), may hold values from -0.21875 to 0.21875
- w_key: bfloat16 [768, 768], P('grp'), may hold values from -0.21875 to 0.21875
- w_value: bfloat16 [768, 768], P('grp'), may hold values from -0.21875 to 0.21875
- w_output: bfloat16 [768, 768], P('grp'), may hold values from -0.625 to 0.625
- position_bias: bfloat16 [384], P('grp'), may hold values from -4 to 300
- ffn_gain: bfloat16 [768], P('grp'), may hold values from 0.5 to 1.5
- expert_up: bfloat16 [8, 3072, 768], P('grp', 'rep'), may hold values from -0.21875 to 0.21875
- expert_down: bfloat16 [8, 3072, 768], P('grp', 'rep'), may hold values from -0.21875 to 0.21875
- cotangent: bfloat16 [4096, 768], P(('rep', 'grp')), may hold values from -6 to 6
Outputs:
- output: bfloat16 [4096, 768], P(('rep', 'grp'))
- input_grad: float32 [4096, 768], P(('rep', 'grp'))
- attn_gain_grad: float32 [768], P('grp')
- w_query_grad: float32 [768, 768], P('grp')
- w_key_grad: float32 [768, 768], P('grp')
- w_value_grad: float32 [768, 768], P('grp')
- w_output_grad: float32 [768, 768], P('grp')
- position_bias_grad: float32 [384], P('grp')
- ffn_gain_grad: float32 [768], P('grp')
- expert_up_grad: float32 [8, 3072, 768], P('grp', 'rep')
- expert_down_grad: float32 [8, 3072, 768], P('grp', 'rep')
The draws below stay inside these ranges and needn't reach their ends.
Inputs may be any that keep to these rules, and one draw needn't show every extreme that they name: `routes`: among the rows of one device no expert is named more than 48 times, a bound that some block reaches. `segment_ids`: each device's row numbers its 4 sequences in order, each 1 to 64 tokens long, one of exactly 64.
All inputs are finite; a program needn't handle non-finite values.
Results may differ from the reference program's by a relative error of at most 0.015.
Values may be sent and summed in bfloat16 or wider, within the bound.
No kernel may reach another device: no remote copies, remote signals or barrier semaphores. Data moves between devices by JAX's collectives and lax.ppermute only.
A program may use at most 128 MiB of HBM per device.

```python
import math
import jax
import jax.numpy as jnp
import numpy as np
from jax import lax

D = 768
H = 12
HD = 64
FF = 3072
NB = 32
SEQS = 4
TOK_DEV = 128
EXPERTS = 8
TOKENS = 4096
SEQ_MOST = 64
CAP = 48
N_REP = 4
N_GRP = 8


def draw_position_bias(key, part):
    base_key = jax.random.fold_in(jax.random.fold_in(key, 7), 0)
    return jnp.clip(jax.random.normal(base_key, (H * NB,), jnp.float32), -4.0, 4.0).astype(jnp.bfloat16)


def plant(drawn, own_key, smallest, largest):
    longest = drawn.shape.index(max(drawn.shape))
    spots = []
    for shift in (0, 1):
        where = [jax.random.randint(jax.random.fold_in(own_key, axis), (), 0, length) for axis, length in enumerate(drawn.shape)]
        where[longest] = (where[longest] + shift) % drawn.shape[longest]
        spots.append(tuple(where))
    return drawn.at[spots[0]].set(smallest).at[spots[1]].set(largest)


def shard_levels(own_key, dims, cuts, least, largest):
    def one(dim, blocks):
        heights = jax.random.uniform(jax.random.fold_in(jax.random.fold_in(own_key, 6), dim), (blocks,), jnp.float32, least / len(cuts), largest / len(cuts))
        return jnp.repeat(jnp.exp(heights), dims[dim] // blocks).reshape((-1,) + (1,) * (len(dims) - dim - 1))

    factor_of = one(*cuts[0])
    for cut in cuts[1:]:
        factor_of = factor_of * one(*cut)
    return factor_of


def split_up(number_of, total, most, slope):
    weights = [(1 << 20) // math.isqrt(standing ** slope) + 1 for standing in range(2, number_of + 1)]
    rest, counts = total - most - (number_of - 1), [1] * (number_of - 1)
    while rest > 0:
        movable = [i for i in range(number_of - 1) if counts[i] < most]
        whole, remaining = sum([weights[i] for i in movable]), rest
        for i in movable:
            extra = min(most - counts[i], max(1, remaining * weights[i] // whole), rest)
            counts[i] = counts[i] + extra
            rest = rest - extra
    return np.array([most] + counts)


def ragged(stream_key, count, total, reach, slope):
    if count == 2:
        one = jax.random.randint(stream_key, (), max(1, total - reach), min(reach, total - 1) + 1)
        return jnp.stack([one, total - one])
    tallies = jnp.asarray(split_up(count, total, reach, slope), jnp.int32)
    pairs = (count - 1) // 2
    donor, taker = tallies[1:1 + 2 * pairs:2], tallies[2:2 + 2 * pairs:2]
    margin = jnp.minimum(donor - 1, reach - taker)
    passed = jax.random.randint(jax.random.fold_in(stream_key, 1), (pairs,), 0, 1 << 20) % (margin + 1)
    tallies = tallies.at[1:1 + 2 * pairs:2].set(donor - passed).at[2:2 + 2 * pairs:2].set(taker + passed)
    return tallies[jax.random.permutation(jax.random.fold_in(stream_key, 2), count)]


def deal_out(own_key, own, number, rows, number_of, top, bound, slope):
    order = jax.random.permutation(own_key, number_of)
    heavy_load, usual = portions_of(number_of, rows * top, bound, slope, True), portions_of(number_of, rows * top, bound, slope, False)
    places = jnp.arange(number_of)

    def named(lengths, turn):
        used = int((lengths > 0).sum())
        fixed = max(1, used // 4)
        moved = fixed + (places - fixed + turn * (used - fixed)) % max(1, number_of - fixed)
        return jnp.zeros((number_of,), jnp.int32).at[order[jnp.where(places < fixed, places, moved)]].set(jnp.asarray(lengths, jnp.int32))

    lengths = jnp.where(number % 4 == 0, named(heavy_load, number // 4), named(usual, number - number // 4 - 1))
    mixed = jax.random.permutation(jax.random.fold_in(own, 3), number_of)
    giver, taker = mixed[0:number_of // 2 * 2:2], mixed[1:number_of // 2 * 2:2]
    slack = jnp.minimum(lengths[giver] - 1, bound - lengths[taker]) // 2
    slack = jnp.where((giver == order[0]) | (taker == order[0]) | (lengths[taker] == 0), 0, jnp.maximum(slack, 0))
    moved = jax.random.randint(jax.random.fold_in(own, 4), (number_of // 2,), 0, 1 << 20) % (slack + 1)
    lengths = lengths.at[giver].add(-moved).at[taker].add(moved)
    labels = jnp.searchsorted(jnp.cumsum(lengths), jnp.arange(rows * top), side="right").astype(jnp.int32)
    grid = labels.reshape(top, rows).T
    grid = grid[jax.random.permutation(jax.random.fold_in(own, 1), rows)]
    turn = jax.random.randint(jax.random.fold_in(own, 2), (rows, 1), 0, top)
    return jnp.take_along_axis(grid, (jnp.arange(top)[None, :] + turn) % top, axis=1)


def portions_of(number_of, total, limit, slope, full):
    portions = [(1 << 20) // math.isqrt(grade ** slope) + 1 for grade in range(1, number_of + 1)]
    largest = limit if full else min(limit, max(-(-total // number_of), total * portions[0] // sum(portions)))
    least = 1 if total - largest >= number_of - 1 else 0
    holding, rest = [largest] + [least] * (number_of - 1), total - largest - least * (number_of - 1)
    while rest > 0:
        free = [i for i in range(1, number_of) if holding[i] < largest] or [i for i in range(1, number_of) if holding[i] < limit]
        whole, left = sum([portions[i] for i in free]), rest
        for i in free:
            extra = min(limit - holding[i], max(1, left * portions[i] // whole), rest)
            holding[i] = holding[i] + extra
            rest = rest - extra
    return np.array(holding)


def gaussian(stream_key, dims, deviation, limit, pieces=(), kind=jnp.bfloat16):
    gain = shard_levels(stream_key, dims, pieces, -0.22, 0.18) if pieces else 1.0
    values = jax.random.normal(stream_key, dims, jnp.float32) * deviation * gain
    return jnp.minimum(jnp.maximum(values, -limit), limit).astype(kind)


def setup_inputs(seed: int = 0) -> dict:
    keys = jax.random.split(jax.random.key(seed), 16)
    tokens = gaussian(keys[0], (TOKENS, D), 1.0, 6.0, ((0, 32),))
    segment_ids = jax.vmap(lambda own: jnp.searchsorted(jnp.cumsum(ragged(own, SEQS, TOK_DEV, SEQ_MOST, 2)), jnp.arange(TOK_DEV), side="right"))(jax.random.split(keys[1], (N_REP * N_GRP))).reshape((N_REP * N_GRP, TOK_DEV)).astype(jnp.int32)
    position_buckets = plant(jax.random.randint(keys[2], (SEQ_MOST,), 0, NB), jax.random.fold_in(keys[2], 1), 0, NB - 1).astype(jnp.int32)
    routes_keys = jax.random.split(jax.random.fold_in(keys[3], 1), TOKENS // TOK_DEV)
    routes_turns = jax.random.permutation(jax.random.fold_in(keys[3], 3), TOKENS // TOK_DEV)
    routes = jax.vmap(lambda own, number: deal_out(jax.random.fold_in(keys[3], 2), own, number, TOK_DEV, EXPERTS, 2, CAP, 2))(routes_keys, routes_turns).reshape((TOKENS, 2))
    gates = jnp.clip(0.1 + 0.79999997 * jax.random.uniform(keys[4], (TOKENS, 2), jnp.float32) ** shard_levels(keys[4], (TOKENS, 2), ((0, 32),), -0.2, 0.2), 0.1, 0.9)
    attn_gain = jnp.clip(1.0 + 0.1 * jax.random.normal(keys[5], (D,), jnp.float32), 0.5, 1.5).astype(jnp.bfloat16)
    w_query = gaussian(keys[6], (D, D), D ** -0.5, 0.21875, ((0, 8),))
    w_key = gaussian(keys[7], (D, D), D ** -0.5, 0.21875, ((0, 8),))
    w_value = gaussian(keys[8], (D, D), D ** -0.5, 0.21875, ((0, 8),))
    w_output = gaussian(keys[9], (D, D), (D // 8) ** -0.5, 0.625, ((0, 8),))
    position_bias = draw_position_bias(jax.random.fold_in(keys[15], 71), 0)
    ffn_gain = jnp.clip(1.0 + 0.1 * jax.random.normal(keys[11], (D,), jnp.float32), 0.5, 1.5).astype(jnp.bfloat16)
    expert_up = gaussian(keys[12], (EXPERTS, FF, D), D ** -0.5, 0.21875, ((0, 8), (1, 4)))
    expert_down = gaussian(keys[13], (EXPERTS, FF, D), (FF // 4) ** -0.5, 0.21875, ((0, 8), (1, 4)))
    cotangent = gaussian(keys[14], (TOKENS, D), 1.0, 6.0, ((0, 32),))
    return {"tokens": tokens, "segment_ids": segment_ids, "position_buckets": position_buckets, "routes": routes, "gates": gates, "attn_gain": attn_gain, "w_query": w_query, "w_key": w_key, "w_value": w_value, "w_output": w_output, "position_bias": position_bias, "ffn_gain": ffn_gain, "expert_up": expert_up, "expert_down": expert_down, "cotangent": cotangent}


EPSILON = 1e-06
MASKED = -1e+30

def rms_forward(values):
    inverse = lax.rsqrt(lax.optimization_barrier(jnp.mean(values * values, axis=-1, keepdims=True)) + EPSILON)
    return (values * inverse, inverse)

def rms_backward(grad_in, normed, inverse, gain_vec):
    gain_grad = lax.optimization_barrier(jnp.sum(grad_in * normed, axis=0))
    scaled = grad_in * gain_vec
    centred = scaled - normed * lax.optimization_barrier(jnp.mean(scaled * normed, axis=-1, keepdims=True))
    return (inverse * centred, gain_grad)

def key_layout(segments, buckets):
    length = segments.shape[0]
    position = jnp.arange(length, dtype=jnp.int32)
    offset = position[:, None] - position[None, :]
    allowed = (segments[:, None] == segments[None, :]) & (offset >= 0)
    index_map = jnp.take(buckets, jnp.clip(offset, 0, buckets.shape[0] - 1).astype(jnp.int32))
    return (index_map, allowed)

def bias_matrix(bias_table, index_map):
    return jnp.take(bias_table, index_map, axis=1)

def split_heads(matrix):
    return matrix.reshape(matrix.shape[0], H, HD).astype(jnp.float32)

def attention_scores(query_rows, key_rows, bias_table, index_map, allowed):
    scores = jnp.einsum('ihd,jhd->hij', split_heads(query_rows), split_heads(key_rows))
    scores = scores * HD ** (-0.5) + bias_matrix(bias_table, index_map)
    return jnp.where(allowed[None], scores, MASKED)

def attention_forward(query_rows, key_rows, value_rows, index_map, allowed, bias_table):
    length = query_rows.shape[0]
    scores = attention_scores(query_rows, key_rows, bias_table, index_map, allowed)
    highest = lax.optimization_barrier(jnp.max(scores, axis=-1, keepdims=True))
    summed = lax.optimization_barrier(jnp.sum(jnp.exp(scores - highest), axis=-1, keepdims=True))
    log_total = highest + jnp.log(summed)
    weights_low = jnp.exp(scores - log_total).astype(jnp.bfloat16)
    mixed = jnp.einsum('hij,jhd->ihd', weights_low.astype(jnp.float32), split_heads(value_rows))
    return (mixed.reshape(length, H * HD).astype(jnp.bfloat16), log_total)

def attention_backward(query_rows, key_rows, value_rows, index_map, allowed, log_total, mixed_grad, bias_table):
    length = query_rows.shape[0]
    scores = attention_scores(query_rows, key_rows, bias_table, index_map, allowed)
    probs = jnp.exp(scores - log_total)
    weights_low = probs.astype(jnp.bfloat16).astype(jnp.float32)
    grad_heads = split_heads(mixed_grad)
    value_grad = jnp.einsum('hij,ihd->jhd', weights_low, grad_heads).reshape(length, H * HD).astype(jnp.bfloat16)
    weight_grad = jnp.einsum('ihd,jhd->hij', grad_heads, split_heads(value_rows))
    centre = lax.optimization_barrier(jnp.sum(probs * weight_grad, axis=-1, keepdims=True))
    score_grad = probs * (weight_grad - centre)
    _, pull_back = jax.vjp(lambda table_in: bias_matrix(table_in, index_map), bias_table)
    table_grad = pull_back(score_grad)[0]
    scaled_low = (score_grad * HD ** (-0.5)).astype(jnp.bfloat16).astype(jnp.float32)
    query_grad = jnp.einsum('hij,jhd->ihd', scaled_low, split_heads(key_rows)).reshape(length, H * HD).astype(jnp.bfloat16)
    key_grad = jnp.einsum('hij,ihd->jhd', scaled_low, split_heads(query_rows)).reshape(length, H * HD).astype(jnp.bfloat16)
    return (query_grad, key_grad, value_grad, table_grad)

def gelu_grad(pre_act, act_grad):
    _, pull_back = jax.vjp(lambda inner: jax.nn.gelu(inner, approximate=True), pre_act)
    return pull_back(act_grad)[0]

def route_ranking(flat_ids):
    matches = (flat_ids[:, None] == jnp.arange(EXPERTS, dtype=jnp.int32)[None, :]).astype(jnp.int32)
    earlier = jnp.cumsum(matches, axis=0) - matches
    return lax.optimization_barrier(jnp.sum(earlier * matches, axis=1)).astype(jnp.int32)

def one_expert(operands):
    rows_in, grads_in, up_weight, down_weight = operands
    pre_act = jnp.dot(rows_in, up_weight.T, preferred_element_type=jnp.float32)
    hidden_act = jax.nn.gelu(pre_act, approximate=True).astype(jnp.bfloat16)
    expert_out = jnp.dot(hidden_act, down_weight, preferred_element_type=jnp.float32).astype(jnp.bfloat16)
    act_grad = jnp.dot(grads_in, down_weight.T, preferred_element_type=jnp.float32)
    pre_grad = gelu_grad(pre_act, act_grad).astype(jnp.bfloat16)
    expert_back = jnp.dot(pre_grad, up_weight, preferred_element_type=jnp.float32).astype(jnp.bfloat16)
    up_grad = jnp.dot(pre_grad.T, rows_in, preferred_element_type=jnp.float32)
    down_grad = jnp.dot(hidden_act.T, grads_in, preferred_element_type=jnp.float32)
    return (expert_out, expert_back, up_grad, down_grad)

def reference(tokens, segment_ids, position_buckets, routes, gates, attn_gain, w_query, w_key, w_value, w_output, position_bias, ffn_gain, expert_up, expert_down, cotangent):
    device_count = N_REP * N_GRP
    inputs = tokens.astype(jnp.float32)
    gain_one = attn_gain.astype(jnp.float32)
    gain_two = ffn_gain.astype(jnp.float32)
    bias_table = position_bias.astype(jnp.float32).reshape(H, NB)
    normed_one, inverse_one = rms_forward(inputs)
    attn_in = (normed_one * gain_one).astype(jnp.bfloat16)
    query_rows = jnp.dot(attn_in, w_query, preferred_element_type=jnp.float32).astype(jnp.bfloat16)
    key_rows = jnp.dot(attn_in, w_key, preferred_element_type=jnp.float32).astype(jnp.bfloat16)
    value_rows = jnp.dot(attn_in, w_value, preferred_element_type=jnp.float32).astype(jnp.bfloat16)
    index_map, allowed = jax.vmap(key_layout, (0, None))(segment_ids, position_buckets)
    per_device = (query_rows.reshape(device_count, TOK_DEV, D), key_rows.reshape(device_count, TOK_DEV, D), value_rows.reshape(device_count, TOK_DEV, D), index_map, allowed)
    mixed, log_total = lax.map(lambda operands: attention_forward(*operands, bias_table), per_device)
    mixed = mixed.reshape(TOKENS, D)
    residual = inputs + jnp.dot(mixed, w_output, preferred_element_type=jnp.float32)
    normed_two, inverse_two = rms_forward(residual)
    ffn_in = (normed_two * gain_two).astype(jnp.bfloat16)
    flat_routes = routes.reshape(device_count, 2 * TOK_DEV)
    ranking = jax.vmap(route_ranking)(flat_routes)
    owners = jnp.arange(device_count, dtype=jnp.int32)[:, None]
    targets = ((flat_routes * device_count + owners) * CAP + ranking).reshape(-1).astype(jnp.int32)
    slot_total = EXPERTS * device_count * CAP
    rows_in = jnp.zeros((slot_total, D), jnp.bfloat16).at[targets].set(jnp.repeat(ffn_in, 2, axis=0))
    out_grad = cotangent.astype(jnp.float32)
    route_grad = (gates[:, :, None] * out_grad[:, None, :]).astype(jnp.bfloat16).reshape(2 * TOKENS, D)
    grads_in = jnp.zeros((slot_total, D), jnp.bfloat16).at[targets].set(route_grad)
    expert_out, expert_back, up_grad, down_grad = lax.map(one_expert, (rows_in.reshape(EXPERTS, device_count * CAP, D), grads_in.reshape(EXPERTS, device_count * CAP, D), expert_up, expert_down))
    picked = expert_out.reshape(slot_total, D)[targets].astype(jnp.float32).reshape(TOKENS, 2, D)
    output = (residual + lax.optimization_barrier(jnp.sum(gates[:, :, None] * picked, axis=1))).astype(jnp.bfloat16)
    ffn_grad = lax.optimization_barrier(jnp.sum(expert_back.reshape(slot_total, D)[targets].astype(jnp.float32).reshape(TOKENS, 2, D), axis=1))
    norm_back, gain_two_grad = rms_backward(ffn_grad, normed_two, inverse_two, gain_two)
    residual_grad = out_grad + norm_back
    residual_low = residual_grad.astype(jnp.bfloat16)
    w_output_grad = jnp.dot(mixed.T, residual_low, preferred_element_type=jnp.float32)
    mixed_grad = jnp.dot(residual_low, w_output.T, preferred_element_type=jnp.float32).astype(jnp.bfloat16)
    per_device_back = per_device + (log_total, mixed_grad.reshape(device_count, TOK_DEV, D))
    query_grad, key_grad, value_grad, table_grad = lax.map(lambda operands: attention_backward(*operands, bias_table), per_device_back)
    query_grad = query_grad.reshape(TOKENS, D)
    key_grad = key_grad.reshape(TOKENS, D)
    value_grad = value_grad.reshape(TOKENS, D)
    table_grad = lax.optimization_barrier(jnp.sum(table_grad, axis=0))
    w_query_grad = jnp.dot(attn_in.T, query_grad, preferred_element_type=jnp.float32)
    w_key_grad = jnp.dot(attn_in.T, key_grad, preferred_element_type=jnp.float32)
    w_value_grad = jnp.dot(attn_in.T, value_grad, preferred_element_type=jnp.float32)
    attn_grad = jnp.dot(query_grad, w_query.T, preferred_element_type=jnp.float32)
    attn_grad = attn_grad + jnp.dot(key_grad, w_key.T, preferred_element_type=jnp.float32)
    attn_grad = attn_grad + jnp.dot(value_grad, w_value.T, preferred_element_type=jnp.float32)
    norm_back_one, gain_one_grad = rms_backward(attn_grad, normed_one, inverse_one, gain_one)
    input_grad = residual_grad + norm_back_one
    return (output, input_grad, gain_one_grad, w_query_grad, w_key_grad, w_value_grad, w_output_grad, table_grad.reshape(-1), gain_two_grad, up_grad, down_grad)
```

```python
import functools

import jax
import jax.numpy as jnp
from jax import lax
from jax.experimental import pallas as pl
from jax.experimental.pallas import tpu as pltpu
from jax.sharding import PartitionSpec as P

H = 12
HD = 64
NB = 32
EPSILON = 1e-06
MASKED = -1e30
F32 = jnp.float32
BF16 = jnp.bfloat16
SMEM = pl.BlockSpec(memory_space=pltpu.SMEM)
VMEM = pl.BlockSpec(memory_space=pltpu.VMEM)


def swap(value, axis, mask):
    size = lax.axis_size(axis)
    return lax.ppermute(value, axis, [(i, i ^ mask) for i in range(size)])


def unxor(parts, index):
    parts = list(parts)
    if len(parts) > 8:
        order = jnp.arange(len(parts), dtype=jnp.int32) ^ index
        return list(jnp.take(jnp.stack(parts), order, axis=0))
    bit = 1
    while bit < len(parts):
        flag = (index & bit) != 0
        parts = [jnp.where(flag, parts[k ^ bit], parts[k]) for k in range(len(parts))]
        bit *= 2
    return parts


def gather_grp(value):
    size = lax.axis_size("grp")
    if size > 8:
        return unxor(list(lax.all_gather(value, "grp")), lax.axis_index("grp"))
    parts = []
    for outer in range(lax.axis_size("grp") // 2):
        one = value if outer == 0 else swap(value, "grp", 2 * outer)
        parts += [one, swap(one, "grp", 1)]
    return parts


def exchange_grp(parts):
    if len(parts) > 8:
        group = lax.axis_index("grp")
        sent = jnp.stack(unxor(parts, group))
        return unxor(list(lax.all_to_all(sent, "grp", 0, 0, tiled=True)), group)
    return [parts[0]] + [swap(parts[k], "grp", k) for k in range(1, len(parts))]


def gather_rep(value):
    half = lax.axis_size("rep") // 2
    near = [value] + [swap(value, "rep", 2 * k) for k in range(1, half)]
    parts = []
    for one in near:
        parts += [one, swap(one, "rep", 1)]
    return parts


def dot(a, b, dims=((1,), (0,)), **kw):
    return lax.dot_general(a, b, (dims, ((), ())), preferred_element_type=F32, **kw)


NT = ((1,), (1,))
TN = ((0,), (0,))


def call(kernel, outs, n_in, scratch=(), **kw):
    return pl.pallas_call(
        kernel,
        out_shape=outs,
        in_specs=[SMEM] + [VMEM] * (n_in - 1),
        out_specs=jax.tree.map(lambda _: VMEM, outs),
        scratch_shapes=scratch,
        **kw,
    )


def shape(dims, dtype):
    return jax.ShapeDtypeStruct(dims, dtype)


def inverse_of(values):
    return lax.rsqrt(jnp.mean(values * values, axis=-1, keepdims=True) + EPSILON)


def slot_hits(slots, total):
    places = lax.broadcasted_iota(jnp.int32, (total, slots.shape[1]), 0)
    return places == slots[0:1, :], places == slots[1:2, :]


def route_kernel(experts, cap, idx, routes, gates, cot, slots, *outs):
    group = idx[0]
    length = routes.shape[1]
    ids = routes[...]
    named = lax.broadcasted_iota(jnp.int32, (experts, length), 0)
    hit0, hit1 = named == ids[0:1, :], named == ids[1:2, :]
    both = jnp.where(hit0, 1.0, 0.0) + jnp.where(hit1, 1.0, 0.0)
    rows = lax.broadcasted_iota(jnp.int32, (length, length), 0)
    cols = lax.broadcasted_iota(jnp.int32, (length, length), 1)
    ahead = jnp.where(rows < cols, 1.0, 0.0).astype(BF16)
    earlier = dot(both.astype(BF16), ahead)
    rank0 = jnp.sum(jnp.where(hit0, earlier, 0.0), axis=0, keepdims=True).astype(jnp.int32)
    rank1 = jnp.sum(jnp.where(hit1, earlier, 0.0), axis=0, keepdims=True).astype(jnp.int32)
    slots[0:1, :] = (ids[0:1, :] ^ group) * cap + rank0
    slots[1:2, :] = (ids[1:2, :] ^ group) * cap + rank1
    at0, at1 = slot_hits(slots[...], experts * cap)
    gate = gates[...]
    weight = jnp.where(at0, gate[0:1, :], 0.0) + jnp.where(at1, gate[1:2, :], 0.0)
    weight = jnp.sum(weight, axis=1, keepdims=True)
    place = (jnp.where(at0, 1.0, 0.0) + jnp.where(at1, 1.0, 0.0)).astype(BF16)
    sent = (dot(place, cot[...]) * weight).astype(BF16)
    for k, out in enumerate(outs):
        out[...] = sent[k * cap : (k + 1) * cap]


def assemble_kernel(idx, *refs):
    *parts, qkv, out = refs
    group = idx[0]
    rows = parts[0].shape[0]
    cols = qkv.shape[1]
    for k, part in enumerate(parts):
        at = pl.ds(pl.multiple_of((group ^ k) * rows, rows), rows)
        qkv[at, :] = part[:, :cols]
        out[at, :] = part[:, cols:]


def skew(line, size):
    wide = jnp.broadcast_to(line, (size, size))
    return pltpu.roll(wide, 0, 1, stride=1, stride_axis=0)


def unskew(values):
    size = values.shape[0]
    rows = lax.broadcasted_iota(jnp.int32, values.shape, 0)
    bit = 1
    while bit < size:
        values = jnp.where((rows & bit) != 0, pltpu.roll(values, size - bit, 1), values)
        bit *= 2
    return values


def allowed_pairs(segs, length):
    named = lax.broadcasted_iota(jnp.int32, (8, length), 0)
    hot = jnp.where(named == segs, 1.0, 0.0).astype(BF16)
    same = dot(hot, hot, TN) > 0.5
    rows = lax.broadcasted_iota(jnp.int32, (length, length), 0)
    cols = lax.broadcasted_iota(jnp.int32, (length, length), 1)
    return same & (rows >= cols)


def attend_kernel(heads, idx, tokens, segs, gain, table, buckets, wqkv, attn_in, qkv, probs, mixed):
    length = tokens.shape[1]
    width = heads * HD
    step = pl.program_id(0)
    values = tokens[0].astype(F32)
    low = (values * inverse_of(values) * gain[...]).astype(BF16)
    attn_in[0] = low
    rows = dot(low, wqkv[...]).astype(BF16)
    qkv[0] = rows
    allowed = allowed_pairs(segs[0], length)
    named = lax.broadcasted_iota(jnp.int32, (NB, length), 0)
    hot = jnp.where(named == buckets[...], 1.0, 0.0).astype(BF16)
    lines = dot(table[...], hot)
    for h in range(heads):
        q = rows[:, h * HD : (h + 1) * HD]
        k = rows[:, width + h * HD : width + (h + 1) * HD]
        v = rows[:, 2 * width + h * HD : 2 * width + (h + 1) * HD]
        scores = dot(q, k, NT) * HD ** (-0.5) + skew(lines[h : h + 1, :], length)
        scores = jnp.where(allowed, scores, MASKED)
        highest = jnp.max(scores, axis=-1, keepdims=True)
        raised = jnp.exp(scores - highest)
        prob = raised / jnp.sum(raised, axis=-1, keepdims=True)
        probs[0, h] = prob
        mixed[0, :, h * HD : (h + 1) * HD] = dot(prob.astype(BF16), v).astype(BF16)


def residual_kernel(cap, idx, mixed, w_out, tokens, gain, slots, residual, *outs):
    total = tokens[...].astype(F32) + dot(mixed[...], w_out[...])
    residual[...] = total
    low = (total * inverse_of(total) * gain[...]).astype(BF16)
    at0, at1 = slot_hits(slots[...], cap * len(outs))
    place = (jnp.where(at0, 1.0, 0.0) + jnp.where(at1, 1.0, 0.0)).astype(BF16)
    sent = dot(place, low).astype(BF16)
    for k, out in enumerate(outs):
        out[...] = sent[k * cap : (k + 1) * cap]


GELU_A = 0.7978845608028654
GELU_B = 0.044715


def expert_kernel(idx, x, grads, up, down, hidden, pre_grad, back, out):
    pre = dot(x[...], up[0], NT)
    act_grad = dot(grads[...], down[0], NT)
    square = pre * pre
    bent = jnp.tanh(GELU_A * (pre + GELU_B * pre * square))
    half = 0.5 * (1.0 + bent)
    slope = half + 0.5 * pre * (1.0 - bent * bent) * (GELU_A * (1.0 + 3.0 * GELU_B * square))
    low = (act_grad * slope).astype(BF16)
    pre_grad[...] = low
    back[...] = dot(low, up[0]).astype(BF16)
    act = (pre * half).astype(BF16)
    hidden[...] = act
    out[...] = dot(act, down[0]).astype(BF16)


def expert_grad_kernel(count, *refs):
    rows, hidden, result = refs[:count], refs[count : 2 * count], refs[2 * count]
    total = dot(hidden[0][...], rows[0][...], TN)
    for k in range(1, count):
        total = total + dot(hidden[k][...], rows[k][...], TN)
    result[0] = total


def add_split_kernel(idx, a, b, *outs):
    total = (a[...].astype(F32) + b[...].astype(F32)).astype(BF16)
    cap = outs[0].shape[0]
    for k, out in enumerate(outs):
        out[...] = total[k * cap : (k + 1) * cap]


def combine_kernel(idx, slots, residual, cot, gain, *refs):
    *parts, grad_out, low_out, gain_grad = refs
    cap = parts[0].shape[0]
    length = residual.shape[0]
    at0, at1 = slot_hits(slots[...], cap * len(parts))
    place = (jnp.where(at0, 1.0, 0.0) + jnp.where(at1, 1.0, 0.0)).astype(BF16)
    rows = jnp.concatenate([part[...] for part in parts], axis=0)
    ffn_grad = dot(place, rows, TN)
    values = residual[...]
    inverse = inverse_of(values)
    normed = values * inverse
    gain_grad[...] = jnp.sum(ffn_grad * normed, axis=0, keepdims=True)
    scaled = ffn_grad * gain[...]
    centred = scaled - normed * jnp.mean(scaled * normed, axis=-1, keepdims=True)
    total = cot[...].astype(F32) + inverse * centred
    grad_out[...] = total
    low_out[...] = total.astype(BF16)


def output_kernel(idx, slots, residual, gates, *refs):
    *parts, out = refs
    cap = parts[0].shape[0]
    at0, at1 = slot_hits(slots[...], cap * len(parts))
    rows = jnp.concatenate([part[...] for part in parts], axis=0)
    first = dot(jnp.where(at0, 1.0, 0.0).astype(BF16), rows, TN)
    second = dot(jnp.where(at1, 1.0, 0.0).astype(BF16), rows, TN)
    gate = gates[...]
    out[...] = (residual[...] + (gate[:, 0:1] * first + gate[:, 1:2] * second)).astype(BF16)


def attend_back_kernel(
    heads, idx, low, w_head, qkv, probs, attn_in, tokens, wqkv, buckets,
    partial, w_grad, gain_grad, table_grad, sums
):
    length = tokens.shape[1]
    width = heads * HD
    step = pl.program_id(0)

    @pl.when(step == 0)
    def _():
        w_grad[...] = jnp.zeros_like(w_grad)
        gain_grad[...] = jnp.zeros_like(gain_grad)
        sums[...] = jnp.zeros_like(sums)

    mixed_grad = dot(low[0], w_head[...], NT).astype(BF16)
    rows = qkv[0]
    grads = [[], [], []]
    for h in range(heads):
        q = rows[:, h * HD : (h + 1) * HD]
        k = rows[:, width + h * HD : width + (h + 1) * HD]
        v = rows[:, 2 * width + h * HD : 2 * width + (h + 1) * HD]
        prob = probs[0, h]
        grad = mixed_grad[:, h * HD : (h + 1) * HD]
        grads[2].append(dot(prob.astype(BF16), grad, TN).astype(BF16))
        weight_grad = dot(grad, v, NT)
        centre = jnp.sum(prob * weight_grad, axis=-1, keepdims=True)
        score_grad = prob * (weight_grad - centre)
        sums[h] += score_grad
        scaled = (score_grad * HD ** (-0.5)).astype(BF16)
        grads[0].append(dot(scaled, k).astype(BF16))
        grads[1].append(dot(scaled, q, TN).astype(BF16))
    joined = jnp.concatenate(grads[0] + grads[1] + grads[2], axis=1)
    w_grad[...] += dot(attn_in[0], joined, TN)
    back = dot(joined, wqkv[...], NT)
    partial[0] = back.astype(BF16)
    values = tokens[0].astype(F32)
    gain_grad[...] += jnp.sum(back * (values * inverse_of(values)), axis=0, keepdims=True)

    @pl.when(step == pl.num_programs(0) - 1)
    def _():
        named = lax.broadcasted_iota(jnp.int32, (NB, length), 0)
        hot = jnp.where(named == buckets[...], 1.0, 0.0)
        table_grad[...] = jnp.zeros_like(table_grad)
        for h in range(heads):
            line = jnp.sum(unskew(sums[h]), axis=0, keepdims=True)
            table_grad[h : h + 1, :NB] = dot(line, hot, NT, precision=lax.Precision.HIGHEST)


def input_kernel(idx, a, b, tokens, gain, residual_grad, result):
    grad = a[...].astype(F32) + b[...].astype(F32)
    values = tokens[...].astype(F32)
    inverse = inverse_of(values)
    normed = values * inverse
    scaled = grad * gain[...]
    centred = scaled - normed * jnp.mean(scaled * normed, axis=-1, keepdims=True)
    result[...] = residual_grad[...] + inverse * centred


def split_rows(values, group, groups):
    pieces = values.reshape(groups, values.shape[0] // groups, values.shape[1])
    return unxor(list(pieces), group)


def scatter_grp(parts):
    even, odd = parts[0::2], parts[1::2]
    arrived = swap(jnp.stack(odd), "grp", 1)
    joined = [(one.astype(F32) + arrived[k].astype(F32)) for k, one in enumerate(even)]
    total = joined[0]
    if len(joined) > 4:
        index = lax.axis_index("grp")
        lines = [[2 * i + half for i in range(len(joined))] for half in range(2)]
        sent = jnp.stack(unxor([one.astype(BF16) for one in joined], index // 2))
        got = lax.all_to_all(sent, "grp", 0, 0, axis_index_groups=lines, tiled=True)
        return jnp.sum(got.astype(F32), axis=0)
    for k in range(1, len(joined)):
        total = total + swap(joined[k].astype(BF16), "grp", 2 * k).astype(F32)
    return total


def local(
    tokens, segment_ids, position_buckets, routes, gates, attn_gain, w_query, w_key, w_value,
    w_output, position_bias, ffn_gain, expert_up, expert_down, cotangent,
):
    length, model = tokens.shape
    groups, reps = lax.axis_size("grp"), lax.axis_size("rep")
    group, rep = lax.axis_index("grp"), lax.axis_index("rep")
    idx = jnp.stack([group, rep]).astype(jnp.int32)
    heads = H // reps
    cols = model // reps
    rows = model // groups
    need = 3 * length // groups
    cap = -(-need // 16) * 16
    slot_total = groups * cap

    pack = jnp.concatenate(
        [lax.dynamic_slice_in_dim(w, rep * cols, cols, 1) for w in (w_query, w_key, w_value, w_output)],
        axis=1,
    )
    weight_parts = gather_grp(pack)
    lanes = 128
    small = jnp.stack(
        [jnp.pad(v, (0, lanes - v.shape[0])) for v in (attn_gain, ffn_gain, position_bias)]
    )
    small_parts = unxor(gather_grp(small), group)
    joined = [
        jnp.concatenate([p[i, : v.shape[0]] for p in small_parts])
        for i, v in enumerate((attn_gain, ffn_gain, position_bias))
    ]
    gain_one = joined[0].astype(F32).reshape(1, model)
    gain_two = joined[1].astype(F32).reshape(1, model)
    table = lax.dynamic_slice_in_dim(joined[2], rep * heads * NB, heads * NB).reshape(heads, NB)
    table = jnp.pad(table, ((0, 8 - heads), (0, 0)))
    far = (length - jnp.arange(length)) % length
    reach = position_buckets.shape[0]
    buckets = jnp.where(far < reach, position_buckets[jnp.minimum(far, reach - 1)], -1)
    buckets = buckets.reshape(1, length)

    token_stack = jnp.stack(gather_rep(tokens))
    segs = jnp.stack(gather_rep(segment_ids))

    routed = call(
        functools.partial(route_kernel, groups, cap),
        [shape((2, length), jnp.int32)] + [shape((cap, model), BF16)] * groups,
        4,
    )(idx, routes.T, gates.T, cotangent)
    slots, grad_chunks = routed[0], routed[1:]

    if rows % 16 == 0:
        wqkv, w_quarter = call(
            assemble_kernel, [shape((model, 3 * cols), BF16), shape((model, cols), BF16)], groups + 1
        )(idx, *weight_parts)
    else:
        whole = jnp.concatenate(unxor(weight_parts, group))
        wqkv, w_quarter = whole[:, : 3 * cols], whole[:, 3 * cols :]
    grad_chunks = lax.optimization_barrier((list(grad_chunks), weight_parts))[0]
    grad_own = jnp.concatenate(exchange_grp(grad_chunks))
    grad_rows = gather_rep(grad_own)

    w_out = jnp.concatenate(unxor(gather_rep(w_quarter), rep), axis=1)

    fixed = lambda dims: pl.BlockSpec(dims, lambda t: (0,) * len(dims))
    per = lambda *dims: pl.BlockSpec((1,) + dims, lambda t: (t,) + (0,) * len(dims))
    attn_in, qkv, probs, mixed_own = pl.pallas_call(
        functools.partial(attend_kernel, heads),
        grid=(reps,),
        in_specs=[
            SMEM, per(length, model), per(1, length), fixed((1, model)), fixed((8, NB)),
            fixed((1, length)), fixed((model, 3 * cols)),
        ],
        out_specs=[
            per(length, model), per(length, 3 * cols), per(heads, length, length), per(length, cols),
        ],
        out_shape=[
            shape((reps, length, model), BF16), shape((reps, length, 3 * cols), BF16),
            shape((reps, heads, length, length), F32), shape((reps, length, cols), BF16),
        ],
    )(idx, token_stack, segs, gain_one, table, buckets, wqkv)

    mixed_parts = gather_rep(mixed_own)
    mixed = jnp.concatenate(unxor([mixed_parts[k][k] for k in range(reps)], rep), axis=1)

    sent = call(
        functools.partial(residual_kernel, cap),
        [shape((length, model), F32)] + [shape((cap, model), BF16)] * groups,
        6,
    )(idx, mixed, w_out, tokens, gain_two, slots)
    residual, row_chunks = sent[0], sent[1:]
    row_own = jnp.concatenate(exchange_grp(list(row_chunks)))
    wide_rows = gather_rep(row_own)

    hidden_units = expert_up.shape[1]
    hidden, pre_grad, back, out = [], [], [], []
    tile = slot_total if slot_total <= 512 else 256
    by_row = pl.BlockSpec((tile, model), lambda t: (t, 0))
    by_unit = pl.BlockSpec((tile, hidden_units), lambda t: (t, 0))
    held = pl.BlockSpec((1, hidden_units, model), lambda t: (0, 0, 0))
    for k in range(reps):
        one = pl.pallas_call(
            expert_kernel,
            grid=(slot_total // tile,),
            in_specs=[SMEM, by_row, by_row, held, held],
            out_specs=[by_unit, by_unit, by_row, by_row],
            out_shape=[shape((slot_total, hidden_units), BF16)] * 2
            + [shape((slot_total, model), BF16)] * 2,
        )(idx, wide_rows[k], grad_rows[k], expert_up, expert_down)
        hidden.append(one[0])
        pre_grad.append(one[1])
        back.append(one[2])
        out.append(one[3])

    def return_rows(parts):
        arrived = [swap(parts[k + 1], "rep", 1) for k in range(0, reps, 2)]
        joined = [
            (parts[2 * k].astype(F32) + arrived[k].astype(F32)).astype(BF16) for k in range(reps // 2)
        ]
        far_part = swap(joined[1], "rep", 2)
        chunks = call(add_split_kernel, [shape((cap, model), BF16)] * groups, 3)(
            idx, joined[0], far_part
        )
        return exchange_grp(list(chunks))

    coming = return_rows(back)
    residual_grad, residual_low, gain_two_grad = call(
        combine_kernel,
        [shape((length, model), F32), shape((length, model), BF16), shape((1, model), F32)],
        5 + groups,
    )(idx, slots, residual, cotangent, gain_two, *coming)

    low_parts = gather_rep(residual_low)
    low_stack = jnp.stack(low_parts)

    returned = return_rows(out)
    output = call(output_kernel, shape((length, model), BF16), 4 + groups)(
        idx, slots, residual, gates, *returned
    )

    def expert_grad(left, right):
        tile = 256
        spec = pl.BlockSpec((slot_total, tile), lambda t: (0, t))
        full = pl.BlockSpec((slot_total, model), lambda t: (0, 0))
        return pl.pallas_call(
            functools.partial(expert_grad_kernel, reps),
            grid=(hidden_units // tile,),
            in_specs=[full] * reps + [spec] * reps,
            out_specs=pl.BlockSpec((1, tile, model), lambda t: (0, t, 0)),
            out_shape=shape((1, hidden_units, model), F32),
        )(*right, *left)

    up_grad = expert_grad(pre_grad, wide_rows)
    down_grad = expert_grad(hidden, grad_rows)

    low_quarter = lax.dynamic_slice_in_dim(low_stack, rep * cols, cols, 2).reshape(-1, cols)
    wo_blocks = []
    for k in range(reps):
        ordered = jnp.concatenate([mixed_parts[k][j ^ k] for j in range(reps)])
        wo_blocks.append(dot(ordered, low_quarter, TN).astype(BF16))
    wo_grad = jnp.concatenate(unxor(wo_blocks, rep))
    wo_owned = scatter_grp(split_rows(wo_grad, group, groups))

    w_head = lax.dynamic_slice_in_dim(w_out, rep * cols, cols, 0)
    partial, wqkv_grad, gain_one_grad, table_grad = pl.pallas_call(
        functools.partial(attend_back_kernel, heads),
        grid=(reps,),
        in_specs=[
            SMEM, per(length, model), fixed((cols, model)), per(length, 3 * cols),
            per(heads, length, length), per(length, model), per(length, model),
            fixed((model, 3 * cols)), fixed((1, length)),
        ],
        out_specs=[
            per(length, model), fixed((model, 3 * cols)), fixed((1, model)), fixed((8, length)),
        ],
        out_shape=[
            shape((reps, length, model), BF16), shape((model, 3 * cols), F32),
            shape((1, model), F32), shape((8, length), F32),
        ],
        scratch_shapes=[pltpu.VMEM((heads, length, length), F32)],
    )(idx, low_stack, w_head, qkv, probs, attn_in, token_stack, wqkv, buckets)

    owned = scatter_grp([p.astype(BF16) for p in split_rows(wqkv_grad, group, groups)])
    mine = jnp.concatenate([owned, wo_owned], axis=1).astype(BF16)
    quarters = unxor(gather_rep(mine), rep)
    dense = [
        jnp.concatenate([q[:, i * cols : (i + 1) * cols] for q in quarters], axis=1).astype(F32)
        for i in range(4)
    ]

    gains = jnp.concatenate([gain_one_grad, gain_two_grad]).reshape(2, groups, rows)
    bias_line = table_grad[:heads, :NB].reshape(1, heads * NB)
    width = max(lanes, heads * NB, rows)
    targets = unxor([gains[:, j] for j in range(groups)], group)
    pads = [jnp.pad(t, ((0, 0), (0, width - rows))) for t in targets]
    bias_row = jnp.pad(bias_line, ((0, 0), (0, width - heads * NB)))
    little = [jnp.concatenate([p, bias_row]) for p in pads]
    total = sum(exchange_grp(little))
    little_parts = gather_rep(total)
    gain_sum = sum(p[:2, :rows] for p in little_parts)
    bias_all = jnp.concatenate([p[2, : heads * NB] for p in unxor(little_parts, rep)])
    share = position_bias.shape[0]
    bias_grad = lax.dynamic_slice_in_dim(bias_all, group * share, share)

    near = [swap(partial[k + 1], "rep", 1) for k in range(0, reps, 2)]
    joined_back = [
        (partial[2 * k].astype(F32) + near[k].astype(F32)).astype(BF16) for k in range(reps // 2)
    ]
    input_grad = call(input_kernel, shape((length, model), F32), 6)(
        idx, joined_back[0], swap(joined_back[1], "rep", 2), tokens, gain_one, residual_grad
    )
    return (
        output, input_grad, gain_sum[0], dense[0], dense[1], dense[2], dense[3], bias_grad,
        gain_sum[1], up_grad, down_grad,
    )


def solution(mesh):
    both = P(("rep", "grp"), None)
    dense = P("grp", None)
    expert = P("grp", "rep", None)
    return jax.shard_map(
        local,
        mesh=mesh,
        in_specs=(
            both, both, P(), both, both, P("grp"), dense, dense, dense, dense, P("grp"), P("grp"),
            expert, expert, both,
        ),
        out_specs=(
            both, both, P("grp"), dense, dense, dense, dense, P("grp"), P("grp"), expert, expert,
        ),
        check_vma=False,
    )
```

```python
import functools

import jax
import jax.numpy as jnp
from jax import lax
from jax.experimental import pallas as pl
from jax.experimental.pallas import tpu as pltpu
from jax.sharding import PartitionSpec as P

H = 12
HD = 64
NB = 32
EPSILON = 1e-06
MASKED = -1e30
F32 = jnp.float32
BF16 = jnp.bfloat16
SMEM = pl.BlockSpec(memory_space=pltpu.SMEM)
VMEM = pl.BlockSpec(memory_space=pltpu.VMEM)


def swap(value, axis, mask):
    size = lax.axis_size(axis)
    return lax.ppermute(value, axis, [(i, i ^ mask) for i in range(size)])


def after(value, *others):
    return lax.optimization_barrier((value, others))[0]


def unxor(parts, index):
    parts = list(parts)
    if len(parts) > 8:
        order = jnp.arange(len(parts), dtype=jnp.int32) ^ index
        return list(jnp.take(jnp.stack(parts), order, axis=0))
    bit = 1
    while bit < len(parts):
        flag = (index & bit) != 0
        parts = [jnp.where(flag, parts[k ^ bit], parts[k]) for k in range(len(parts))]
        bit *= 2
    return parts


def gather_grp(value):
    size = lax.axis_size("grp")
    if size > 8:
        return unxor(list(lax.all_gather(value, "grp")), lax.axis_index("grp"))
    parts = []
    for outer in range(lax.axis_size("grp") // 2):
        one = value if outer == 0 else swap(value, "grp", 2 * outer)
        parts += [one, swap(one, "grp", 1)]
    return parts


def exchange_grp(parts, late=(), gate=()):
    if late and len(parts) <= 8:
        held = after([parts[k] for k in late], gate)
        parts = [held[late.index(k)] if k in late else parts[k] for k in range(len(parts))]
    if len(parts) > 8:
        group = lax.axis_index("grp")
        sent = jnp.stack(unxor(parts, group))
        return unxor(list(lax.all_to_all(sent, "grp", 0, 0, tiled=True)), group)
    return [parts[0]] + [swap(parts[k], "grp", k) for k in range(1, len(parts))]


def gather_rep(value):
    half = lax.axis_size("rep") // 2
    near = [value] + [swap(value, "rep", 2 * k) for k in range(1, half)]
    parts = []
    for one in near:
        parts += [one, swap(one, "rep", 1)]
    return parts


def dot(a, b, dims=((1,), (0,)), **kw):
    return lax.dot_general(a, b, (dims, ((), ())), preferred_element_type=F32, **kw)


NT = ((1,), (1,))
TN = ((0,), (0,))


def call(kernel, outs, n_in, scratch=(), **kw):
    return pl.pallas_call(
        kernel,
        out_shape=outs,
        in_specs=[SMEM] + [VMEM] * (n_in - 1),
        out_specs=jax.tree.map(lambda _: VMEM, outs),
        scratch_shapes=scratch,
        **kw,
    )


def shape(dims, dtype):
    return jax.ShapeDtypeStruct(dims, dtype)


def inverse_of(values):
    return lax.rsqrt(jnp.mean(values * values, axis=-1, keepdims=True) + EPSILON)


def slot_hits(slots, total):
    places = lax.broadcasted_iota(jnp.int32, (total, slots.shape[1]), 0)
    return places == slots[0:1, :], places == slots[1:2, :]


def route_kernel(experts, cap, idx, routes, gates, cot, slots, *outs):
    group = idx[0]
    length = routes.shape[1]
    ids = routes[...]
    named = lax.broadcasted_iota(jnp.int32, (experts, length), 0)
    hit0, hit1 = named == ids[0:1, :], named == ids[1:2, :]
    both = jnp.where(hit0, 1.0, 0.0) + jnp.where(hit1, 1.0, 0.0)
    rows = lax.broadcasted_iota(jnp.int32, (length, length), 0)
    cols = lax.broadcasted_iota(jnp.int32, (length, length), 1)
    ahead = jnp.where(rows < cols, 1.0, 0.0).astype(BF16)
    earlier = dot(both.astype(BF16), ahead)
    rank0 = jnp.sum(jnp.where(hit0, earlier, 0.0), axis=0, keepdims=True).astype(jnp.int32)
    rank1 = jnp.sum(jnp.where(hit1, earlier, 0.0), axis=0, keepdims=True).astype(jnp.int32)
    slots[0:1, :] = (ids[0:1, :] ^ group) * cap + rank0
    slots[1:2, :] = (ids[1:2, :] ^ group) * cap + rank1
    at0, at1 = slot_hits(slots[...], experts * cap)
    gate = gates[...]
    weight = jnp.where(at0, gate[0:1, :], 0.0) + jnp.where(at1, gate[1:2, :], 0.0)
    weight = jnp.sum(weight, axis=1, keepdims=True)
    place = (jnp.where(at0, 1.0, 0.0) + jnp.where(at1, 1.0, 0.0)).astype(BF16)
    sent = (dot(place, cot[...]) * weight).astype(BF16)
    for k, out in enumerate(outs):
        out[...] = sent[k * cap : (k + 1) * cap]


def choose(parts, index):
    bit = 1
    while len(parts) > 1:
        flag = (index & bit) != 0
        parts = [jnp.where(flag, parts[i + 1], parts[i]) for i in range(0, len(parts), 2)]
        bit *= 2
    return parts[0]


def pack_kernel(base, reps, idx, w_query, w_key, w_value, w_output, *refs):
    *lines, out, spare = refs
    rows, model = w_query.shape
    cols = model // reps
    for i, w in enumerate((w_query, w_key, w_value, w_output)):
        quarter = choose([w[:, q * cols : (q + 1) * cols] for q in range(reps)], idx[1])
        out[:rows, i * cols : (i + 1) * cols] = quarter
    spare[...] = jnp.zeros_like(spare)
    for i, line in enumerate(lines):
        spare[i : i + 1, : line.shape[1]] = line[...].astype(F32)
    out[base : base + 8, :] = spare[...].astype(BF16)


def small_kernel(reps, heads, share, rows, idx, small, gains, table, line):
    groups = small.shape[0]
    for j in range(groups):
        block = small[j].astype(F32)
        gains[:, j * rows : (j + 1) * rows] = block[:, :rows]
        line[0:1, j * share : (j + 1) * share] = block[2:3, :share]
    span = heads * NB
    mine = choose([line[0:1, q * span : (q + 1) * span] for q in range(reps)], idx[1])
    table[...] = jnp.zeros_like(table)
    for h in range(heads):
        table[h : h + 1, :] = mine[:, h * NB : (h + 1) * NB]


def assemble_kernel(rows, base, reps, heads, share, idx, *refs):
    *parts, qkv, out, gains, table, small, line = refs
    group = idx[0]
    cols = qkv.shape[1]
    for k, part in enumerate(parts):
        at = pl.ds(pl.multiple_of((group ^ k) * rows, rows), rows)
        qkv[at, :] = part[:rows, :cols]
        out[at, :] = part[:rows, cols:]
        small[group ^ k] = part[base : base + 8, : small.shape[2]].astype(F32)
    small_kernel(reps, heads, share, rows, idx, small, gains, table, line)


def skew(line, size):
    wide = jnp.broadcast_to(line, (size, size))
    return pltpu.roll(wide, 0, 1, stride=1, stride_axis=0)


def unskew(values):
    size = values.shape[0]
    rows = lax.broadcasted_iota(jnp.int32, values.shape, 0)
    bit = 1
    while bit < size:
        values = jnp.where((rows & bit) != 0, pltpu.roll(values, size - bit, 1), values)
        bit *= 2
    return values


def allowed_pairs(segs, length):
    named = lax.broadcasted_iota(jnp.int32, (8, length), 0)
    hot = jnp.where(named == segs, 1.0, 0.0).astype(BF16)
    same = dot(hot, hot, TN) > 0.5
    rows = lax.broadcasted_iota(jnp.int32, (length, length), 0)
    cols = lax.broadcasted_iota(jnp.int32, (length, length), 1)
    return same & (rows >= cols)


def attend_kernel(heads, idx, tokens, segs, gain, table, buckets, wqkv, attn_in, qkv, probs, mixed):
    length = tokens.shape[1]
    width = heads * HD
    step = pl.program_id(0)
    values = tokens[0].astype(F32)
    low = (values * inverse_of(values) * gain[0:1, :]).astype(BF16)
    attn_in[0] = low
    rows = dot(low, wqkv[...]).astype(BF16)
    qkv[0] = rows
    allowed = allowed_pairs(segs[0], length)
    named = lax.broadcasted_iota(jnp.int32, (NB, length), 0)
    hot = jnp.where(named == buckets[...], 1.0, 0.0).astype(BF16)
    lines = dot(table[...].astype(BF16), hot)
    for h in range(heads):
        q = rows[:, h * HD : (h + 1) * HD]
        k = rows[:, width + h * HD : width + (h + 1) * HD]
        v = rows[:, 2 * width + h * HD : 2 * width + (h + 1) * HD]
        scores = dot(q, k, NT) * HD ** (-0.5) + skew(lines[h : h + 1, :], length)
        scores = jnp.where(allowed, scores, MASKED)
        highest = jnp.max(scores, axis=-1, keepdims=True)
        raised = jnp.exp(scores - highest)
        prob = raised / jnp.sum(raised, axis=-1, keepdims=True)
        probs[0, h] = prob
        mixed[0, :, h * HD : (h + 1) * HD] = dot(prob.astype(BF16), v).astype(BF16)


def residual_kernel(cap, reps, idx, tokens, gain, slots, *refs):
    mixed, w_out, (residual, *outs, spare) = refs[:reps], refs[reps : 2 * reps], refs[2 * reps :]
    cols = w_out[0].shape[1]
    rep = idx[1]
    for j, block in enumerate(unxor([m[k] for k, m in enumerate(mixed)], rep)):
        spare[:, j * cols : (j + 1) * cols] = block
    whole = spare[...]
    for j, block in enumerate(unxor([dot(whole, w[...]) for w in w_out], rep)):
        at = slice(j * cols, (j + 1) * cols)
        residual[:, at] = tokens[:, at].astype(F32) + block
    total = residual[...]
    low = (total * inverse_of(total) * gain[1:2, :]).astype(BF16)
    at0, at1 = slot_hits(slots[...], cap * len(outs))
    place = (jnp.where(at0, 1.0, 0.0) + jnp.where(at1, 1.0, 0.0)).astype(BF16)
    sent = dot(place, low).astype(BF16)
    for k, out in enumerate(outs):
        out[...] = sent[k * cap : (k + 1) * cap]


GELU_A = 0.7978845608028654
GELU_B = 0.044715


def expert_kernel(idx, x, grads, up, down, hidden, pre_grad, back):
    pre = dot(x[...], up[0], NT)
    act_grad = dot(grads[...], down[0], NT)
    square = pre * pre
    bent = jnp.tanh(GELU_A * (pre + GELU_B * pre * square))
    half = 0.5 * (1.0 + bent)
    slope = half + 0.5 * pre * (1.0 - bent * bent) * (GELU_A * (1.0 + 3.0 * GELU_B * square))
    low = (act_grad * slope).astype(BF16)
    pre_grad[...] = low
    back[...] = dot(low, up[0]).astype(BF16)
    hidden[...] = (pre * half).astype(BF16)


def expert_out_kernel(reps, idx, down, *refs):
    for k in range(reps):
        refs[reps + k][...] = dot(refs[k][...], down[0]).astype(BF16)


def expert_grad_kernel(count, *refs):
    rows, hidden, result = refs[:count], refs[count : 2 * count], refs[2 * count]
    total = dot(hidden[0][...], rows[0][...], TN)
    for k in range(1, count):
        total = total + dot(hidden[k][...], rows[k][...], TN)
    result[0] = total


def add_split_kernel(first, idx, a, b, *outs):
    size = b.shape[0]
    total = (a[first : first + size].astype(F32) + b[...].astype(F32)).astype(BF16)
    cap = outs[0].shape[0]
    for k, out in enumerate(outs):
        out[...] = total[k * cap : (k + 1) * cap]


def combine_kernel(idx, slots, residual, cot, gain, *refs):
    *parts, grad_out, low_out, gain_grad = refs
    cap = parts[0].shape[0]
    length = residual.shape[0]
    at0, at1 = slot_hits(slots[...], cap * len(parts))
    place = (jnp.where(at0, 1.0, 0.0) + jnp.where(at1, 1.0, 0.0)).astype(BF16)
    rows = jnp.concatenate([part[...] for part in parts], axis=0)
    ffn_grad = dot(place, rows, TN)
    values = residual[...]
    inverse = inverse_of(values)
    normed = values * inverse
    gain_grad[...] = jnp.sum(ffn_grad * normed, axis=0, keepdims=True)
    scaled = ffn_grad * gain[1:2, :]
    centred = scaled - normed * jnp.mean(scaled * normed, axis=-1, keepdims=True)
    total = cot[...].astype(F32) + inverse * centred
    grad_out[...] = total
    low_out[...] = total.astype(BF16)


def output_kernel(idx, slots, residual, gates, *refs):
    *parts, out = refs
    cap = parts[0].shape[0]
    at0, at1 = slot_hits(slots[...], cap * len(parts))
    rows = jnp.concatenate([part[...] for part in parts], axis=0)
    first = dot(jnp.where(at0, 1.0, 0.0).astype(BF16), rows, TN)
    second = dot(jnp.where(at1, 1.0, 0.0).astype(BF16), rows, TN)
    gate = gates[...]
    out[...] = (residual[...] + (gate[:, 0:1] * first + gate[:, 1:2] * second)).astype(BF16)


def attend_back_kernel(
    heads, reps, groups, idx, qkv, probs, tokens, attn_in, wqkv, buckets, ffn_gain_grad, *refs
):
    w_out, mixed, lows = refs[:reps], refs[reps : 2 * reps], refs[2 * reps : 3 * reps]
    partial, even, odd, w_head, joined, grads_all, gains, sums, mixed_grads = refs[3 * reps :]
    length = tokens.shape[1]
    width = heads * HD
    step = pl.program_id(0)
    group, rep = idx[0], idx[1]

    @pl.when(step == 0)
    def _():
        head = pl.ds(pl.multiple_of(rep * width, width), width)
        for j, block in enumerate(unxor([w[head, :] for w in w_out], rep)):
            w_head[:, j * width : (j + 1) * width] = block
        gains[...] = jnp.zeros_like(gains)
        gains[1:2, :] = ffn_gain_grad[...]
        sums[...] = jnp.zeros_like(sums)
        for j, low in enumerate(lows):
            mixed_grads[j] = dot(low[...], w_head[...], NT).astype(BF16)

    mixed_grad = mixed_grads[step]
    rows = qkv[0]
    here = pl.ds(pl.multiple_of(step * length, length), length)
    grads = [[], [], []]
    for h in range(heads):
        q = rows[:, h * HD : (h + 1) * HD]
        k = rows[:, width + h * HD : width + (h + 1) * HD]
        v = rows[:, 2 * width + h * HD : 2 * width + (h + 1) * HD]
        prob = probs[0, h]
        grad = mixed_grad[:, h * HD : (h + 1) * HD]
        weight_grad = dot(grad, v, NT)
        centre = jnp.sum(prob * weight_grad, axis=-1, keepdims=True)
        score_grad = prob * (weight_grad - centre)
        sums[h] += score_grad
        scaled = (score_grad * HD ** (-0.5)).astype(BF16)
        grads[0].append(dot(scaled, k).astype(BF16))
        grads[1].append(dot(scaled, q, TN).astype(BF16))
        grads[2].append(dot(prob.astype(BF16), grad, TN).astype(BF16))
    both = jnp.concatenate(grads[0] + grads[1] + grads[2], axis=1)
    joined[here, :] = both
    back = dot(both, wqkv[...], NT)
    partial[0] = back.astype(BF16)
    values = tokens[0].astype(F32)
    gains[0:1, :] += jnp.sum(back * (values * inverse_of(values)), axis=0, keepdims=True)

    @pl.when(step == pl.num_programs(0) - 1)
    def _():
        model = tokens.shape[2]
        attended = attn_in[...].reshape(reps * length, model)
        grads_all[:, : 3 * width] = dot(attended, joined[...], TN)
        quarter = jnp.concatenate(
            [
                choose([low[:, j * width : (j + 1) * width] for j in range(reps)], rep)
                for low in lows
            ],
            axis=0,
        )
        for k in range(reps):
            ordered = jnp.concatenate([mixed[k][j ^ k] for j in range(reps)], axis=0)
            at = pl.ds(pl.multiple_of((rep ^ k) * width, width), width)
            grads_all[at, 3 * width :] = dot(ordered, quarter, TN)
        named = lax.broadcasted_iota(jnp.int32, (NB, length), 0)
        hot = jnp.where(named == buckets[...], 1.0, 0.0)
        for h in range(heads):
            line = jnp.sum(unskew(sums[h]), axis=0, keepdims=True)
            gains[2 + h : 3 + h, :NB] = dot(line, hot, NT, precision=lax.Precision.HIGHEST)
        share = model // groups
        base = -(-share // 16) * 16
        heads_part = gains[2:8, :NB]
        for k in range(groups):
            out = odd if k % 2 else even
            if share % 8 == 0:
                at = pl.ds(pl.multiple_of((group ^ k) * share, share), share)
                block = grads_all[at, :]
                pair = choose([gains[0:2, j * share : (j + 1) * share] for j in range(groups)], group ^ k)
            else:
                block = grads_all[k * share : (k + 1) * share, :]
                pair = gains[0:2, k * share : (k + 1) * share]
            out[k // 2, :share, :] = block.astype(BF16)
            spare = jnp.concatenate(
                [
                    jnp.pad(pair, ((0, 0), (0, 128 - share))),
                    jnp.pad(heads_part, ((0, 0), (0, 128 - NB))),
                ],
                axis=0,
            )
            out[k // 2, base : base + 8, :128] = spare.astype(BF16)


def half_sum_kernel(idx, even, arrived, *outs):
    for k, out in enumerate(outs):
        out[...] = (even[k].astype(F32) + arrived[k].astype(F32)).astype(BF16)


def total_kernel(idx, *refs):
    *parts, out = refs
    total = parts[0][...].astype(F32)
    for part in parts[1:]:
        total = total + part[...].astype(F32)
    out[...] = total.astype(BF16)


def finish_kernel(reps, heads, rows, base, idx, *refs):
    parts, outs = refs[:reps], refs[reps:]
    cols = parts[0].shape[1] // 4
    small = [part[base : base + 8, :128].astype(F32) for part in parts]
    for j, part in enumerate(unxor([part[...] for part in parts], idx[1])):
        for i in range(4):
            outs[i][:, j * cols : (j + 1) * cols] = part[:rows, i * cols : (i + 1) * cols].astype(F32)
    total = small[0]
    for one in small[1:]:
        total = total + one
    outs[4][...] = total[0:1, :rows]
    outs[5][...] = total[1:2, :rows]
    line = outs[7]
    for j, one in enumerate(unxor(small, idx[1])):
        for h in range(heads):
            at = (j * heads + h) * NB
            line[0:1, at : at + NB] = one[2 + h : 3 + h, :NB]
    share = outs[6].shape[1]
    outs[6][...] = choose([line[0:1, q * share : (q + 1) * share] for q in range(H * NB // share)], idx[0])


def input_kernel(idx, a, b, tokens, gain, residual_grad, result):
    grad = a[...].astype(F32) + b[...].astype(F32)
    values = tokens[...].astype(F32)
    inverse = inverse_of(values)
    normed = values * inverse
    scaled = grad * gain[0:1, :]
    centred = scaled - normed * jnp.mean(scaled * normed, axis=-1, keepdims=True)
    result[...] = residual_grad[...] + inverse * centred


def cost(flops, size, exps=0):
    return pl.CostEstimate(flops=flops, bytes_accessed=size, transcendentals=exps)


def local(
    tokens, segment_ids, position_buckets, routes, gates, attn_gain, w_query, w_key, w_value,
    w_output, position_bias, ffn_gain, expert_up, expert_down, cotangent,
):
    length, model = tokens.shape
    groups, reps = lax.axis_size("grp"), lax.axis_size("rep")
    group, rep = lax.axis_index("grp"), lax.axis_index("rep")
    idx = jnp.stack([group, rep]).astype(jnp.int32)
    heads = H // reps
    cols = model // reps
    rows = model // groups
    base = -(-rows // 16) * 16
    need = 3 * length // groups
    cap = -(-need // 16) * 16
    slot_total = groups * cap
    lanes = 128
    share = position_bias.shape[0]

    lines = [v.reshape(1, -1) for v in (attn_gain, ffn_gain, position_bias)]
    pack = call(
        functools.partial(pack_kernel, base, reps), shape((base + 8, model), BF16), 5 + len(lines),
        [pltpu.VMEM((8, model), F32)],
    )(idx, w_query, w_key, w_value, w_output, *lines)
    weight_parts = gather_grp(pack)
    token_parts = gather_rep(after(tokens, pack))

    far = (length - jnp.arange(length)) % length
    reach = position_buckets.shape[0]
    buckets = jnp.where(far < reach, position_buckets[jnp.minimum(far, reach - 1)], -1)
    buckets = buckets.reshape(1, length)

    token_stack = jnp.stack(token_parts)
    segs = jnp.stack(gather_rep(after(segment_ids, pack)))

    routed = call(
        functools.partial(route_kernel, groups, cap),
        [shape((2, length), jnp.int32)] + [shape((cap, model), BF16)] * groups,
        4,
    )(idx, routes.T, gates.T, cotangent)
    slots = routed[0]
    grad_chunks = after(list(routed[1:]), weight_parts[::2] + weight_parts[3:4])
    weight_parts = after(weight_parts, token_stack, segs, buckets)
    if rows % 16 == 0:
        wqkv, w_quarter, gains, table = call(
            functools.partial(assemble_kernel, rows, base, reps, heads, share),
            [
                shape((model, 3 * cols), BF16), shape((model, cols), BF16),
                shape((8, model), F32), shape((8, NB), F32),
            ],
            groups + 1,
            [pltpu.VMEM((groups, 8, lanes), F32), pltpu.VMEM((8, H * NB), F32)],
        )(idx, *weight_parts)
    else:
        ordered = unxor(weight_parts, group)
        whole = jnp.concatenate([p[:rows] for p in ordered])
        wqkv, w_quarter = whole[:, : 3 * cols], whole[:, 3 * cols :]
        small = jnp.stack([p[base : base + 8, :lanes] for p in ordered])
        gains, table = call(
            functools.partial(small_kernel, reps, heads, share, rows),
            [shape((8, model), F32), shape((8, NB), F32)], 2, [pltpu.VMEM((8, H * NB), F32)],
        )(idx, small)
    w_parts = gather_rep(w_quarter)

    fixed = lambda *dims: pl.BlockSpec(dims, lambda t: (0,) * len(dims))
    per = lambda *dims: pl.BlockSpec((1,) + dims, lambda t: (t,) + (0,) * len(dims))
    attn_in, qkv, probs, mixed_own = pl.pallas_call(
        functools.partial(attend_kernel, heads),
        grid=(reps,),
        in_specs=[
            SMEM, per(length, model), per(1, length), fixed(8, model), fixed(8, NB),
            fixed(1, length), fixed(model, 3 * cols),
        ],
        out_specs=[
            per(length, model), per(length, 3 * cols), per(heads, length, length), per(length, cols),
        ],
        out_shape=[
            shape((reps, length, model), BF16), shape((reps, length, 3 * cols), BF16),
            shape((reps, heads, length, length), F32), shape((reps, length, cols), BF16),
        ],
        cost_estimate=cost(2 * reps * length * model * 3 * cols, 8 << 20, reps * heads * length**2),
    )(idx, token_stack, segs, gains, table, buckets, wqkv)
    mixed_parts = gather_rep(mixed_own)
    grad_own = jnp.concatenate(exchange_grp(grad_chunks, (4, 5, 6, 7), mixed_own))

    sent = call(
        functools.partial(residual_kernel, cap, reps),
        [shape((length, model), F32)] + [shape((cap, model), BF16)] * groups,
        4 + 2 * reps,
        [pltpu.VMEM((length, model), BF16)],
    )(idx, tokens, gains, slots, *mixed_parts, *w_parts)
    residual, row_chunks = sent[0], sent[1:]
    row_own = jnp.concatenate(exchange_grp(list(row_chunks)))
    grad_rows = gather_rep(grad_own)
    wide_rows = [row_own, swap(row_own, "rep", 1)]

    hidden_units = expert_up.shape[1]
    hidden, pre_grad, back = [], [], []
    tile = slot_total if slot_total <= 512 else 256
    by_row = pl.BlockSpec((tile, model), lambda t: (t, 0))
    by_unit = pl.BlockSpec((tile, hidden_units), lambda t: (t, 0))
    held = pl.BlockSpec((1, hidden_units, model), lambda t: (0, 0, 0))
    work = 2 * slot_total * hidden_units * model
    for k in range(reps):
        if k % 2 == 0 and k:
            far = after(swap(row_own, "rep", k), back)
            wide_rows += [far, swap(far, "rep", 1)]
        one = pl.pallas_call(
            expert_kernel,
            grid=(slot_total // tile,),
            in_specs=[SMEM, by_row, by_row, held, held],
            out_specs=[by_unit, by_unit, by_row],
            out_shape=[shape((slot_total, hidden_units), BF16)] * 2 + [shape((slot_total, model), BF16)],
            cost_estimate=cost(3 * work, 6 << 20, slot_total * hidden_units),
        )(idx, wide_rows[k], grad_rows[k], expert_up, expert_down)
        hidden.append(one[0])
        pre_grad.append(one[1])
        back.append(one[2])

    half_rows, half_groups = slot_total // 2, groups // 2

    def reduce_near(parts):
        arrived = [swap(parts[k + 1], "rep", 1) for k in range(0, reps, 2)]
        near = (parts[0].astype(F32) + arrived[0].astype(F32)).astype(BF16)
        far = [
            (parts[2][i : i + half_rows].astype(F32) + arrived[1][i : i + half_rows].astype(F32)).astype(
                BF16
            )
            for i in (0, half_rows)
        ]
        return near, far

    def reduce_far(near, far, *others):
        moved = [None, swap(far[1], "rep", 2)]
        moved[0] = after(swap(far[0], "rep", 2), *others)
        chunks = [None, None]
        for i in (1, 0):
            chunks[i] = list(
                call(
                    functools.partial(add_split_kernel, i * half_rows),
                    [shape((cap, model), BF16)] * half_groups, 3,
                )(idx, near, moved[i])
            )
        return chunks[0] + chunks[1]

    back_near, back_far = reduce_near(back)
    outs = call(
        functools.partial(expert_out_kernel, reps),
        [shape((slot_total, model), BF16)] * reps,
        2 + reps,
        cost_estimate=cost(reps * work, 6 << 20),
    )(idx, expert_down, *after(hidden, back_far))
    out_near, out_far = reduce_near(outs)
    back_chunks = reduce_far(back_near, back_far, out_near, out_far)
    out_chunks = reduce_far(out_near, after(out_far, back_chunks[0]))
    coming = after(exchange_grp(back_chunks), out_chunks)
    residual_grad, residual_low, gain_two_grad = call(
        combine_kernel,
        [shape((length, model), F32), shape((length, model), BF16), shape((1, model), F32)],
        5 + groups,
    )(idx, slots, residual, cotangent, gains, *coming)

    def expert_grad(left, right):
        unit = 256
        spec = pl.BlockSpec((slot_total, unit), lambda t: (0, t))
        full = pl.BlockSpec((slot_total, model), lambda t: (0, 0))
        return pl.pallas_call(
            functools.partial(expert_grad_kernel, reps),
            grid=(hidden_units // unit,),
            in_specs=[full] * reps + [spec] * reps,
            out_specs=pl.BlockSpec((1, unit, model), lambda t: (0, t, 0)),
            out_shape=shape((1, hidden_units, model), F32),
            cost_estimate=cost(reps * work, 8 << 20),
        )(*right, *left)

    low_parts = gather_rep(residual_low)
    out_chunks = after(out_chunks, residual_low)

    chunk = (base + 8, model)
    partial, even, odd = pl.pallas_call(
        functools.partial(attend_back_kernel, heads, reps, groups),
        grid=(reps,),
        in_specs=[
            SMEM, per(length, 3 * cols), per(heads, length, length), per(length, model),
            fixed(reps, length, model), fixed(model, 3 * cols), fixed(1, length), fixed(1, model),
        ]
        + [fixed(model, cols)] * reps
        + [fixed(reps, length, cols)] * reps
        + [fixed(length, model)] * reps,
        out_specs=[per(length, model)] + [fixed(groups // 2, *chunk)] * 2,
        out_shape=[shape((reps, length, model), BF16)] + [shape((groups // 2, *chunk), BF16)] * 2,
        scratch_shapes=[
            pltpu.VMEM((cols, model), BF16), pltpu.VMEM((reps * length, 3 * cols), BF16),
            pltpu.VMEM((model, model), F32), pltpu.VMEM((8, model), F32),
            pltpu.VMEM((heads, length, length), F32), pltpu.VMEM((reps, length, cols), BF16),
        ],
        cost_estimate=cost(6 * reps * length * model * 3 * cols, 12 << 20),
    )(
        idx, qkv, probs, token_stack, attn_in, wqkv, buckets, gain_two_grad, *w_parts, *mixed_parts,
        *low_parts,
    )

    if rows % 8:
        natural = [(even, odd)[k % 2][k // 2] for k in range(groups)]
        swapped = unxor(natural, group)
        even, odd = jnp.stack(swapped[0::2]), jnp.stack(swapped[1::2])
    arrived = swap(odd, "grp", 1)
    returned = exchange_grp(out_chunks, (2, 4, 6), odd)
    near = [swap(partial[k + 1], "rep", 1) for k in range(0, reps, 2)]
    joined_back = [
        (partial[2 * k].astype(F32) + near[k].astype(F32)).astype(BF16) for k in range(reps // 2)
    ]
    far_back = swap(joined_back[1], "rep", 2)
    up_grad = expert_grad(after(pre_grad, odd), wide_rows)
    down_grad = expert_grad(after(hidden, odd), grad_rows)
    even = after(even, returned, joined_back, up_grad, down_grad)
    def last_parts(*gate):
        parts = after(returned, *gate)
        output = call(output_kernel, shape((length, model), BF16), 4 + groups)(
            idx, slots, residual, gates, *parts
        )
        input_grad = call(input_kernel, shape((length, model), F32), 6)(
            idx, joined_back[0], after(far_back, *gate), tokens, gains, residual_grad
        )
        return output, input_grad

    if groups > 8:
        joined = even.astype(F32) + arrived.astype(F32)
        side = [[2 * i + half for i in range(groups // 2)] for half in range(2)]
        moved = jnp.stack(unxor(list(joined.astype(BF16)), group // 2))
        moved = lax.all_to_all(moved, "grp", 0, 0, axis_index_groups=side, tiled=True)
        mine = jnp.sum(moved.astype(F32), axis=0).astype(BF16)
        output, input_grad = last_parts()
    else:
        joined = call(half_sum_kernel, [shape(chunk, BF16)] * (groups // 2), 3)(idx, even, arrived)
        output, input_grad = last_parts(joined)
        moved = [joined[0]] + [swap(joined[k], "grp", 2 * k) for k in range(1, groups // 2)]
        moved = after(moved, output, input_grad)
        mine = call(total_kernel, shape(chunk, BF16), 1 + len(moved))(idx, *moved)
    finished = call(
        functools.partial(finish_kernel, reps, heads, rows, base),
        [shape((rows, model), F32)] * 4 + [shape((1, rows), F32)] * 2 + [shape((1, share), F32)],
        1 + reps,
        [pltpu.VMEM((8, H * NB), F32)],
    )(idx, *gather_rep(mine))
    dense, small_grads = finished[:4], [one.reshape(-1) for one in finished[4:]]

    return (
        output, input_grad, small_grads[0], *dense, small_grads[2], small_grads[1], up_grad, down_grad,
    )


def solution(mesh):
    both = P(("rep", "grp"), None)
    dense = P("grp", None)
    expert = P("grp", "rep", None)
    return jax.shard_map(
        local,
        mesh=mesh,
        in_specs=(
            both, both, P(), both, both, P("grp"), dense, dense, dense, dense, P("grp"), P("grp"),
            expert, expert, both,
        ),
        out_specs=(
            both, both, P("grp"), dense, dense, dense, dense, P("grp"), P("grp"), expert, expert,
        ),
        check_vma=False,
    )
```
